32 devices in a mesh: rep: 8 (over z, y), shard: 4 (over x, core).
Axes of the slice: x: 2, y: 2, z: 4, core: 2. Of those that a mesh axis runs over, the one named last changes fastest.
Arguments:
- hidden_in: bfloat16 [32768, 1024], P(('rep', 'shard')), may hold values from -6 to 6
- teacher: bfloat16 [32768, 1024], P(('rep', 'shard')), may hold values from -6 to 6
- cotangent: bfloat16 [32768, 1024], P(('rep', 'shard')), may hold values from -6 to 6
- lengths: int32 [32], P(('rep', 'shard')), may hold values from 512 to 1024, as said below
- norm_attn: float32 [1024], replicated, may hold values from 0.5 to 1.5
- w_in: bfloat16 [1024, 6144], P('shard'), may hold values from -0.1875 to 0.1875
- w_small: bfloat16 [1024, 24], P('shard'), may hold values from -0.1875 to 0.1875
- conv_w: float32 [4, 5120], replicated, may hold values from -3 to 3
- a_log: float32 [8], replicated, may hold values from -6 to 0.5
- dt_bias: float32 [8], replicated, may hold values from -2 to 1
- norm_head: float32 [128], replicated, may hold values from 0.5 to 1.5
- w_out: bfloat16 [1024, 1024], P('shard'), may hold values from -0.1875 to 0.1875
- norm_mlp: float32 [1024], replicated, may hold values from 0.5 to 1.5
- w_mlp_in: bfloat16 [1024, 5632], P('shard'), may hold values from -0.1875 to 0.1875
- w_mlp_down: bfloat16 [2816, 1024], P('shard'), may hold values from -0.109375 to 0.109375
Outputs:
- layer_out: bfloat16 [32768, 1024], P(('rep', 'shard'))
- loss: float32 [], replicated
- grad_hidden: bfloat16 [32768, 1024], P(('rep', 'shard'))
- grad_norm_attn: float32 [1024], replicated
- grad_w_in: float32 [1024, 6144], P('shard')
- grad_w_small: float32 [1024, 24], P('shard')
- grad_conv_w: float32 [4, 5120], replicated
- grad_a_log: float32 [8], replicated
- grad_dt_bias: float32 [8], replicated
- grad_norm_head: float32 [128], replicated
- grad_w_out: float32 [1024, 1024], P('shard')
- grad_norm_mlp: float32 [1024], replicated
- grad_w_mlp_in: float32 [1024, 5632], P('shard')
- grad_w_mlp_down: float32 [2816, 1024], P('shard')
The draws below stay inside these ranges and needn't reach their ends.
Inputs may be any that keep to these rules, and one draw needn't show every extreme that they name: `lengths`: each sequence's valid slots are a prefix of its 1024 slots; in every draw some sequence is full and some holds 512 valid slots.
All inputs are finite; a program needn't handle non-finite values.
Results may differ from the reference program's by a relative error of at most 0.014.
Values may be sent and summed in bfloat16 or wider, within the bound.
No kernel may reach another device: no remote copies, remote signals or barrier semaphores. Data moves between devices by JAX's collectives and lax.ppermute only.
A program may use at most 512 MiB of HBM per device.

```python
import math
import jax
import jax.numpy as jnp
from jax import lax

D = 1024
HEADS = 8
DK = 128
DV = 128
HOUSE = 2
FF = 2816
CONV = 4
BLOCK = 64
LEN = 1024
PROJ = 6144
SMALLW = 24
CONVCH = 5120
SEQS = 32
TOKENS = 32768


def draw_lengths(key, part):
    drawn_lengths = jax.random.randint(key, (SEQS,), LEN // 2, LEN + 1)
    marker = jnp.arange(SEQS)
    drawn_lengths = jnp.where(marker == 0, LEN, drawn_lengths)
    drawn_lengths = jnp.where(marker == 1, LEN // 2, drawn_lengths)
    return drawn_lengths.astype(jnp.int32)


def shard_levels(own_key, extent, cuts, smallest, high):
    def one(dim, parts):
        draws = jax.random.uniform(jax.random.fold_in(jax.random.fold_in(own_key, 6), dim), (parts,), jnp.float32, smallest / len(cuts), high / len(cuts))
        return jnp.repeat(jnp.exp(draws), extent[dim] // parts).reshape((-1,) + (1,) * (len(extent) - dim - 1))

    factor_of = one(*cuts[0])
    for cut in cuts[1:]:
        factor_of = factor_of * one(*cut)
    return factor_of


def bell_draw(stream_key, dims, scale, limit, split=(), kind=jnp.bfloat16):
    loudness = shard_levels(stream_key, dims, split, -0.22, 0.18) if split else 1.0
    result = jax.random.normal(stream_key, dims, jnp.float32) * scale * loudness
    return jnp.minimum(jnp.maximum(result, -limit), limit).astype(kind)


def setup_inputs(seed: int = 0) -> dict:
    key_of = jax.random.split(jax.random.key(seed), 16)
    return {
        "hidden_in": bell_draw(key_of[0], (TOKENS, D), 1.0, 6.0, ((0, 32),)),
        "teacher": bell_draw(key_of[1], (TOKENS, D), 1.0, 6.0, ((0, 32),)),
        "cotangent": bell_draw(key_of[2], (TOKENS, D), 1.0, 6.0, ((0, 32),)),
        "lengths": draw_lengths(jax.random.fold_in(key_of[15], 71), 0),
        "norm_attn": jnp.clip(1.0 + 0.1 * jax.random.normal(key_of[4], (D,), jnp.float32), 0.5, 1.5),
        "w_in": bell_draw(key_of[5], (D, PROJ), D ** -0.5, 0.1875, ((0, 4),)),
        "w_small": bell_draw(key_of[6], (D, SMALLW), D ** -0.5, 0.1875, ((0, 4),)),
        "conv_w": bell_draw(key_of[7], (CONV, CONVCH), 0.5, 3.0, (), jnp.float32),
        "a_log": jnp.clip(jax.random.uniform(key_of[8], (HEADS,), jnp.float32, -6.0, 0.5), -6.0, 0.5),
        "dt_bias": jnp.clip(jax.random.uniform(key_of[9], (HEADS,), jnp.float32, -2.0, 1.0), -2.0, 1.0),
        "norm_head": jnp.clip(1.0 + 0.1 * jax.random.normal(key_of[10], (DV,), jnp.float32), 0.5, 1.5),
        "w_out": bell_draw(key_of[11], (HEADS * DV, D), (HEADS * DV) ** -0.5, 0.1875, ((0, 4),)),
        "norm_mlp": jnp.clip(1.0 + 0.1 * jax.random.normal(key_of[12], (D,), jnp.float32), 0.5, 1.5),
        "w_mlp_in": bell_draw(key_of[13], (D, 2 * FF), D ** -0.5, 0.1875, ((0, 4),)),
        "w_mlp_down": bell_draw(key_of[14], (FF, D), FF ** -0.5, 0.109375, ((0, 4),)),
    }


EPSILON = 1e-06
PRECISE = lax.Precision.HIGHEST

@jax.custom_vjp
def low(v):
    return lax.optimization_barrier(v.astype(jnp.bfloat16)).astype(jnp.float32)

@jax.custom_vjp
def low_back(v):
    return v

def low_keep(v):
    return (low(v), None)

def low_pass(kept, grad):
    return (grad,)

def back_keep(v):
    return (v, None)

def back_low(kept, grad):
    return (low(grad),)
low.defvjp(low_keep, low_pass)
low_back.defvjp(back_keep, back_low)

def norm_rows(row_values, gain_row):
    return row_values * lax.rsqrt(lax.optimization_barrier(jnp.mean(row_values * row_values, axis=-1, keepdims=True)) + EPSILON) * gain_row

def block_coupling(keys_in, beta_rows, log_gates):
    row_count = keys_in.shape[0]
    cumulated = jnp.cumsum(log_gates, axis=0).T
    keys_head = jnp.transpose(keys_in, (1, 0, 2))
    betas_head = beta_rows.T
    row_index = lax.broadcasted_iota(jnp.int32, (row_count, row_count), 0)
    col_index = lax.broadcasted_iota(jnp.int32, (row_count, row_count), 1)
    strictly = (col_index < row_index)[None]
    spread_log = cumulated[:, :, None] - cumulated[:, None, :]
    fading = jnp.where(strictly, jnp.exp(jnp.where(strictly, spread_log, 0.0)), 0.0)
    intersections = jnp.einsum('hrc,hic->hri', keys_head, keys_head, precision=PRECISE)
    return intersections * fading * betas_head[:, None, :]

def block_step(memory, pieces):
    queries, keys_in, values_in, beta_rows, log_gates, inverse = pieces
    row_count = keys_in.shape[0]
    query_count = queries.shape[0]
    substeps = row_count // query_count
    cumulated = jnp.cumsum(log_gates, axis=0).T
    keys_head = jnp.transpose(keys_in, (1, 0, 2))
    values_head = jnp.transpose(values_in, (1, 0, 2))
    queries_head = jnp.transpose(queries, (1, 0, 2))
    betas_head = beta_rows.T
    carried = jnp.einsum('hrc,hcd->hrd', keys_head, memory, precision=PRECISE)
    targets = values_head - jnp.exp(cumulated)[:, :, None] * carried
    updates = jnp.einsum('hri,hid->hrd', inverse, targets, precision=PRECISE)
    read_row = lax.broadcasted_iota(jnp.int32, (query_count, row_count), 0) * substeps + substeps - 1
    read_col = lax.broadcasted_iota(jnp.int32, (query_count, row_count), 1)
    visible = (read_col <= read_row)[None]
    read_log = cumulated[:, substeps - 1::substeps]
    query_spread = read_log[:, :, None] - cumulated[:, None, :]
    query_fading = jnp.where(visible, jnp.exp(jnp.where(visible, query_spread, 0.0)), 0.0)
    scores = jnp.einsum('htc,hic->hti', queries_head, keys_head, precision=PRECISE) * query_fading * betas_head[:, None, :]
    outputs = jnp.exp(read_log)[:, :, None] * jnp.einsum('htc,hcd->htd', queries_head, memory, precision=PRECISE)
    outputs = outputs + jnp.einsum('hti,hid->htd', scores, updates, precision=PRECISE)
    last_log = cumulated[:, -1]
    carry_weights = jnp.exp(last_log[:, None] - cumulated) * betas_head
    new_memory = jnp.exp(last_log)[:, None, None] * memory + jnp.einsum('hic,hid->hcd', keys_head * carry_weights[:, :, None], updates, precision=PRECISE)
    return (new_memory, jnp.transpose(outputs, (1, 0, 2)))

def sequence_mix(queries, keys_in, values_in, beta_rows, log_gates):
    block_count = queries.shape[0] // BLOCK
    memory = jnp.zeros((HEADS, DK, DV), jnp.float32)
    keys_blocks = keys_in.reshape(block_count, BLOCK * HOUSE, HEADS, DK)
    beta_blocks = beta_rows.reshape(block_count, BLOCK * HOUSE, HEADS)
    gate_blocks = log_gates.reshape(block_count, BLOCK * HOUSE, HEADS)
    coupling = jax.vmap(block_coupling)(keys_blocks, beta_blocks, gate_blocks)
    identity = jnp.broadcast_to(jnp.eye(BLOCK * HOUSE, dtype=jnp.float32), coupling.shape)
    inverse = lax.linalg.triangular_solve(coupling, identity, left_side=True, lower=True, unit_diagonal=True)
    pieces = (queries.reshape(block_count, BLOCK, HEADS, DK), keys_blocks, values_in.reshape(block_count, BLOCK * HOUSE, HEADS, DV), beta_blocks, gate_blocks, inverse)
    final_memory, outputs = lax.scan(jax.checkpoint(block_step), memory, pieces)
    return outputs.reshape(queries.shape[0], HEADS, DV)

def mixer_core(proj_rows, small_rows, conv_w, a_log, dt_bias, norm_head):
    slot_count = proj_rows.shape[0]
    tap_count = conv_w.shape[0]
    channel_count = conv_w.shape[1]
    conv_input = proj_rows[:, :channel_count]
    padded = jnp.concatenate([jnp.zeros((tap_count - 1, channel_count), jnp.float32), conv_input], axis=0)
    conv_out = conv_w[0] * padded[0:slot_count]
    for offset in range(1, tap_count):
        conv_out = conv_out + conv_w[offset] * padded[offset:offset + slot_count]
    active = jax.nn.silu(conv_out)
    query_width = HEADS * DK
    key_width = HOUSE * HEADS * DK
    queries = active[:, :query_width].reshape(slot_count, HEADS, DK)
    keys_in = active[:, query_width:query_width + key_width].reshape(slot_count * HOUSE, HEADS, DK)
    values_in = active[:, query_width + key_width:].reshape(slot_count * HOUSE, HEADS, DV)
    queries = queries * lax.rsqrt(lax.optimization_barrier(jnp.sum(queries * queries, axis=-1, keepdims=True)) + EPSILON) * DK ** (-0.5)
    keys_in = keys_in * lax.rsqrt(lax.optimization_barrier(jnp.sum(keys_in * keys_in, axis=-1, keepdims=True)) + EPSILON)
    beta_rows = jax.nn.sigmoid(small_rows[:, :HOUSE * HEADS]).reshape(slot_count * HOUSE, HEADS)
    decays = -jnp.exp(a_log) * jax.nn.softplus(small_rows[:, HOUSE * HEADS:] + dt_bias)
    log_gates = jnp.concatenate([decays[:, None, :], jnp.zeros((slot_count, HOUSE - 1, HEADS), jnp.float32)], axis=1).reshape(slot_count * HOUSE, HEADS)
    mixed_heads = sequence_mix(queries, keys_in, values_in, beta_rows, log_gates)
    mixed_heads = mixed_heads * lax.rsqrt(lax.optimization_barrier(jnp.mean(mixed_heads * mixed_heads, axis=-1, keepdims=True)) + EPSILON) * norm_head
    out_gate = proj_rows[:, channel_count:].reshape(slot_count, HEADS, DV)
    return (mixed_heads * jax.nn.silu(out_gate)).reshape(slot_count, HEADS * DV)

def layer(hidden, norm_attn, w_in, w_small, conv_w, a_log, dt_bias, norm_head, w_out, norm_mlp, w_mlp_in, w_mlp_down):
    row_count = hidden.shape[0]
    seq_group = row_count // LEN
    normed_in = low(norm_rows(hidden, norm_attn))
    proj_rows = low_back(jnp.dot(normed_in, w_in, precision=PRECISE))
    small_rows = low_back(jnp.dot(normed_in, w_small, precision=PRECISE))
    mixed_rows = jax.vmap(mixer_core, in_axes=(0, 0, None, None, None, None))(proj_rows.reshape(seq_group, LEN, PROJ), small_rows.reshape(seq_group, LEN, SMALLW), conv_w, a_log, dt_bias, norm_head)
    mixed_rows = mixed_rows.reshape(row_count, HEADS * DV)
    attended = low_back(jnp.dot(low(mixed_rows), w_out, precision=PRECISE))
    residual = hidden + attended
    normed_mid = low(norm_rows(residual, norm_mlp))
    gate_up = low_back(jnp.dot(normed_mid, w_mlp_in, precision=PRECISE))
    product = low(jax.nn.silu(gate_up[:, :FF]) * gate_up[:, FF:])
    return residual + low_back(jnp.dot(product, w_mlp_down, precision=PRECISE))

def reference(hidden_in, teacher, cotangent, lengths, norm_attn, w_in, w_small, conv_w, a_log, dt_bias, norm_head, w_out, norm_mlp, w_mlp_in, w_mlp_down):
    params = (norm_attn.astype(jnp.float32), w_in.astype(jnp.float32), w_small.astype(jnp.float32), conv_w.astype(jnp.float32), a_log.astype(jnp.float32), dt_bias.astype(jnp.float32), norm_head.astype(jnp.float32), w_out.astype(jnp.float32), norm_mlp.astype(jnp.float32), w_mlp_in.astype(jnp.float32), w_mlp_down.astype(jnp.float32))
    seq_total = lengths.shape[0]
    per_group = math.gcd(seq_total, max(1, 4096 // LEN))
    group_count = seq_total // per_group
    group_rows = per_group * LEN
    stacked = (hidden_in.reshape(group_count, group_rows, D), teacher.reshape(group_count, group_rows, D), cotangent.reshape(group_count, group_rows, D), lengths.reshape(group_count, per_group))

    def one_group(running_state, group_item):
        grad_sums, loss_sum = running_state
        hidden_rows, teacher_rows, cot_rows, group_lengths = group_item

        def forward_rows(hidden_part, norm_a, w_a, w_b, conv_part, log_part, bias_part, head_part, w_c, norm_b, w_d, w_e):
            return layer(hidden_part, norm_a, w_a, w_b, conv_part, log_part, bias_part, head_part, w_c, norm_b, w_d, w_e)
        out_rows, pull_back = jax.vjp(forward_rows, hidden_rows.astype(jnp.float32), params[0], params[1], params[2], params[3], params[4], params[5], params[6], params[7], params[8], params[9], params[10])
        slot_index = lax.broadcasted_iota(jnp.int32, (per_group, LEN), 1)
        valid_rows = (slot_index < group_lengths[:, None]).astype(jnp.float32).reshape(group_rows, 1)
        deviation = out_rows - teacher_rows.astype(jnp.float32)
        gradients = pull_back(valid_rows * (cot_rows.astype(jnp.float32) + deviation))
        grad_sums = jax.tree.map(lambda running, addend: running + addend, grad_sums, tuple(gradients[1:]))
        loss_sum = loss_sum + jnp.sum(valid_rows * deviation * deviation)
        return ((grad_sums, loss_sum), (out_rows.astype(jnp.bfloat16), gradients[0].astype(jnp.bfloat16)))
    zero_sums = jax.tree.map(jnp.zeros_like, params)
    (grad_sums, loss_sum), (out_all, dx_all) = lax.scan(one_group, (zero_sums, jnp.zeros((), jnp.float32)), stacked)
    valid_count = jnp.sum(lengths).astype(jnp.float32)
    loss_value = loss_sum / (valid_count * D)
    return (out_all.reshape(TOKENS, D), loss_value, dx_all.reshape(TOKENS, D), grad_sums[0], grad_sums[1], grad_sums[2], grad_sums[3], grad_sums[4], grad_sums[5], grad_sums[6], grad_sums[7], grad_sums[8], grad_sums[9], grad_sums[10])
```

```python
import functools

import jax
import jax.numpy as jnp
from jax import lax
from jax.experimental import pallas as pl
from jax.experimental.pallas import tpu as pltpu
from jax.sharding import PartitionSpec as P

HEADS = 8
DK = 128
HOUSE = 2
BLOCK = 64
HB = 4
GROUPS = HEADS // HB
EPSILON = 1e-06
EPS = EPSILON
f32 = jnp.float32
bf16 = jnp.bfloat16


def norm_rows(row_values, gain_row):
    return (
        row_values
        * lax.rsqrt(jnp.mean(row_values * row_values, axis=-1, keepdims=True) + EPSILON)
        * gain_row
    )


def dot_plain(a,b): return nn(a,b)
def dot_right_t(a,b): return nt(a,b)
def dot_left_t(a,b): return tn(a,b)
def nn(a,b): return lax.dot_general(a,b,(((1,),(0,)),((),())),preferred_element_type=f32)
def nt(a,b): return lax.dot_general(a,b,(((1,),(1,)),((),())),preferred_element_type=f32)
def tn(a,b): return lax.dot_general(a,b,(((0,),(0,)),((),())),preferred_element_type=f32)
def lo(x): return x.astype(bf16)
def sigmoid(x): return 0.5*jnp.tanh(0.5*x)+0.5
def cat(*xs): return jnp.concatenate(xs,axis=0)

def token_masks(C):
    row=lax.broadcasted_iota(jnp.int32,(C,2*C),0)
    col=lax.broadcasted_iota(jnp.int32,(C,2*C),1)
    left=col<C
    tok=jnp.where(left,col,col-C)
    return row,tok,left

def gates(colg,rowg,h,HB,C):
    c_col=colg[:,h:h+1]
    c_row=rowg[h:h+1,:]
    b_row=rowg[HB+h:HB+h+1,:]
    return c_col,c_row,b_row

def fwd_body(C,HB,x_ref,cw_ref,colg_ref,rowg_ref,nh_ref,mixed_ref,o_ref,s0_ref,t_ref,u_ref,xs,S):
    W=HB*128
    CV=5*W
    @pl.when(pl.program_id(2)==0)
    def _():
        xs[0:8,:]=jnp.zeros((8,CV),f32)
        S[...]=jnp.zeros_like(S)
    @pl.when(pl.program_id(2)!=0)
    def _():
        xs[0:8,:]=xs[C:C+8,:]
    xs[8:8+C,:]=x_ref[:,0:CV].astype(f32)
    row,tok,left=token_masks(C)
    incl=tok<=row
    strict=tok<row
    botm=tok<row+jnp.where(left,1,0)
    colg=colg_ref[...]
    rowg=rowg_ref[0]
    eye=jnp.where((tok==row)&left,1.0,0.0)
    eye2=jnp.where((tok==row)&jnp.logical_not(left),1.0,0.0)
    pair=jnp.where((tok==row)&left,1.0,0.0)
    def act(slot,h):
        sl=slice(slot*W+h*128,slot*W+h*128+128)
        y=cw_ref[3:4,sl]*xs[8:8+C,sl]
        for i in range(3):
            y=y+cw_ref[i:i+1,sl]*xs[5+i:5+i+C,sl]
        return y*sigmoid(y)
    def l2(a): return a*lax.rsqrt(jnp.sum(a*a,axis=-1,keepdims=True)+EPS)
    H=range(HB)
    Q=[];K=[];V=[];E=[];G3=[]
    for h in H:
        q=l2(act(0,h))*(128**-0.5)
        k=cat(l2(act(1,h)),l2(act(2,h)))
        Q.append(q);K.append(k)
        V.append(cat(act(3,h),act(4,h)))
    Y=[lo(cat(Q[h],K[h])) for h in H]
    Kb=[lo(K[h]) for h in H]
    GP=[nt(Y[h],Kb[h]) for h in H]
    A=[];M=[];CC=[]
    for h in H:
        c_col,c_row,b_row=gates(colg,rowg,h,HB,C)
        e=jnp.exp(jnp.minimum(c_col-c_row,0.0))*b_row
        M.append(lo(jnp.where(incl,GP[h][0:C]*e,0.0)))
        A.append(cat(jnp.where(strict,GP[h][C:2*C]*e,0.0),jnp.where(botm,GP[h][2*C:3*C]*e,0.0)))
    T=[cat(eye,eye2-A[h][C:2*C]*pair) for h in H]
    s=1
    while s<C:
        m=((tok//(2*s))==(row//(2*s)))&((row//s)%2==1)&((tok//s)%2==0)
        mf=jnp.where(m,1.0,0.0)
        Tb=[lo(T[h]) for h in H]
        Z=[nn(lo(cat(A[h][0:C]*mf,A[h][C:2*C]*mf)),Tb[h]) for h in H]
        T=[T[h]-nn(Tb[h],lo(Z[h])) for h in H]
        s*=2
    Tb=[lo(T[h]) for h in H]
    S0=[S[:,h*128:h*128+128] for h in H]
    S0b=[lo(S0[h]) for h in H]
    YS=[nn(Y[h],S0b[h]) for h in H]
    U=[]
    for h in H:
        c_col=colg[:,h:h+1]
        ec=jnp.exp(c_col)
        ks=YS[h][C:3*C]
        R=V[h]-cat(ec*ks[0:C],ec*ks[C:2*C])
        U.append(lo(nn(Tb[h],lo(R))))
    for h in H:
        sl=slice(h*128,h*128+128)
        c_col=colg[:,h:h+1]
        ec=jnp.exp(c_col)
        O=ec*YS[h][0:C]+nn(M[h],U[h])
        cl=colg[C-1:C,h:h+1]
        ew=jnp.exp(cl-c_col)
        w0=ew*colg[:,HB+h:HB+h+1]
        w1=ew*colg[:,2*HB+h:2*HB+h+1]
        kw=lo(cat(w0*K[h][0:C],w1*K[h][C:2*C]))
        S[:,sl]=jnp.exp(cl)*S0[h]+tn(kw,U[h])
        s0_ref[0,:,sl]=S0b[h]
        t_ref[0,:,sl]=Tb[h]
        u_ref[0,:,sl]=U[h]
        o_ref[:,sl]=O
        g=x_ref[:,CV+h*128:CV+h*128+128].astype(f32)
        r=lax.rsqrt(jnp.mean(O*O,axis=-1,keepdims=True)+EPS)
        mixed_ref[:,sl]=lo(O*r*nh_ref[...]*(g*sigmoid(g)))

def mixer_fwd(x,cw,colg,rowg,nh,nseq):
    C=BLOCK
    R=x.shape[0]; nch=R//nseq//C; W=HB*128; ng=GROUPS
    rb=lambda g,s,n:(s*nch+n,g)
    cb=lambda g,s,n:(s*nch+n,0,g)
    NC=nseq*nch
    return pl.pallas_call(
        functools.partial(fwd_body,C,HB),
        grid=(ng,nseq,nch),
        in_specs=[pl.BlockSpec((C,6*W),rb),pl.BlockSpec((4,5*W),lambda g,s,n:(0,g)),
                  pl.BlockSpec((C,128),rb),pl.BlockSpec((1,2*HB,128),lambda g,s,n:(s*nch+n,g,0)),
                  pl.BlockSpec((1,128),lambda g,s,n:(0,0))],
        out_specs=[pl.BlockSpec((C,W),rb),pl.BlockSpec((C,W),rb),
                   pl.BlockSpec((1,128,W),cb),pl.BlockSpec((1,128,W),cb),pl.BlockSpec((1,128,W),cb)],
        out_shape=[jax.ShapeDtypeStruct((R,ng*W),bf16),jax.ShapeDtypeStruct((R,ng*W),f32),
                   jax.ShapeDtypeStruct((NC,128,ng*W),bf16),jax.ShapeDtypeStruct((NC,128,ng*W),bf16),jax.ShapeDtypeStruct((NC,128,ng*W),bf16)],
        scratch_shapes=[pltpu.VMEM((C+8,5*W),f32),pltpu.VMEM((128,W),f32)],
        compiler_params=pltpu.CompilerParams(dimension_semantics=("arbitrary",)*3,vmem_limit_bytes=48<<20),
        name="mixer_fwd",
    )(x,cw,colg,rowg,nh)

def bwd_body(C,HB,x_ref,xp_ref,cw_ref,colg_ref,rowg_ref,nh_ref,gm_ref,o_ref,s0_ref,t_ref,u_ref,
             gx_ref,col_ref,row_ref,dcw_ref,dnh_ref,xs,gs,dS):
    W=HB*128
    CV=5*W
    n=pl.program_id(2); nch=pl.num_programs(2)
    first=(pl.program_id(1)==0)&(n==0)
    @pl.when(first)
    def _():
        dcw_ref[...]=jnp.zeros_like(dcw_ref)
        dnh_ref[...]=jnp.zeros_like(dnh_ref)
    @pl.when(n==0)
    def _():
        gs[C:C+8,:]=jnp.zeros((8,CV),f32)
        dS[...]=jnp.zeros_like(dS)
    @pl.when(n!=0)
    def _():
        gs[C:C+8,:]=gs[0:8,:]
    @pl.when(n==nch-1)
    def _():
        xs[0:8,:]=jnp.zeros((8,CV),f32)
    @pl.when(n!=nch-1)
    def _():
        xs[0:8,:]=xp_ref[:,0:CV].astype(f32)
    xs[8:8+C,:]=x_ref[:,0:CV].astype(f32)
    row,tok,left=token_masks(C)
    incl=tok<=row
    strict=tok<row
    botm=tok<row+jnp.where(left,1,0)
    colg=colg_ref[...]
    rowg=rowg_ref[0]
    lane=lax.broadcasted_iota(jnp.int32,(C,128),1)
    H=range(HB)
    def conv(slot,h):
        sl=slice(slot*W+h*128,slot*W+h*128+128)
        y=cw_ref[3:4,sl]*xs[8:8+C,sl]
        for i in range(3):
            y=y+cw_ref[i:i+1,sl]*xs[5+i:5+i+C,sl]
        return y
    def act_norm(slot,h):
        y=conv(slot,h)
        sg=sigmoid(y)
        a=y*sg
        r=lax.rsqrt(jnp.sum(a*a,axis=-1,keepdims=True)+EPS)
        dsil=sg*(1.0+y*(1.0-sg))
        return a*r,r,dsil
    Q=[];K=[];rq=[];rk0=[];rk1=[];dq_s=[];dk0_s=[];dk1_s=[]
    for h in H:
        a,r,d=act_norm(0,h); Q.append(a*(128**-0.5)); rq.append(r); dq_s.append(d)
        a0,r0,d0=act_norm(1,h); a1,r1,d1=act_norm(2,h)
        K.append(cat(a0,a1)); rk0.append(r0); rk1.append(r1); dk0_s.append(d0); dk1_s.append(d1)
    dO=[]
    nhg=nh_ref[...]
    for h in H:
        sl=slice(h*128,h*128+128)
        O=o_ref[:,sl]; gm=gm_ref[:,sl].astype(f32)
        gt=x_ref[:,CV+h*128:CV+h*128+128].astype(f32)
        sg=sigmoid(gt)
        r=lax.rsqrt(jnp.mean(O*O,axis=-1,keepdims=True)+EPS)
        on=O*r
        gsil=gm*(gt*sg)
        t1=gsil*on
        dnh_ref[0]+=jnp.sum(t1.reshape(C//8,8,128),axis=0)
        dgt=gm*(on*nhg)*(sg*(1.0+gt*(1.0-sg)))
        gx_ref[:,CV+h*128:CV+h*128+128]=lo(dgt)
        u=gsil*nhg
        dO.append(r*(u-on*jnp.mean(u*on,axis=-1,keepdims=True)))
    Y=[cat(Q[h],K[h]) for h in H]
    Yb=[lo(y) for y in Y]
    Kb=[lo(K[h]) for h in H]
    GP=[nt(Yb[h],Kb[h]) for h in H]
    dU=[];Eq=[];EA=[];dSb=[];ecs=[];ews=[]
    for h in H:
        sl=slice(h*128,h*128+128)
        c_col,c_row,b_row=gates(colg,rowg,h,HB,C)
        e=jnp.exp(jnp.minimum(c_col-c_row,0.0))
        eq=jnp.where(incl,e,0.0); ea=cat(jnp.where(strict,e,0.0),jnp.where(botm,e,0.0))
        Eq.append(eq);EA.append(ea)
        M=lo(GP[h][0:C]*eq*b_row)
        cl=colg[C-1:C,h:h+1]
        ec=jnp.exp(c_col); ew=jnp.exp(cl-c_col)
        ecs.append(ec);ews.append(ew)
        w0=ew*colg[:,HB+h:HB+h+1]
        w1=ew*colg[:,2*HB+h:2*HB+h+1]
        kw=lo(cat(w0*K[h][0:C],w1*K[h][C:2*C]))
        db_=lo(dS[:,sl]); dSb.append(db_)
        dU.append(lo(tn(M,lo(dO[h]))+nn(kw,db_)))
    dR=[tn(t_ref[0,:,h*128:h*128+128],dU[h]) for h in H]
    dAM=[nt(lo(cat(dO[h],-dR[h])),u_ref[0,:,h*128:h*128+128]) for h in H]
    Z=[]
    for h in H:
        ec=ecs[h]
        Z.append(lo(cat(ec*dO[h],-(ec*dR[h][0:C]),-(ec*dR[h][C:2*C]))))
    UdS=[nt(u_ref[0,:,h*128:h*128+128],dSb[h]) for h in H]
    colout=jnp.zeros((C,128),f32)
    rows=[]
    X=[]
    ZS=[nt(Z[h],s0_ref[0,:,h*128:h*128+128]) for h in H]
    for h in H:
        sl=slice(h*128,h*128+128)
        cl=colg[C-1:C,h:h+1]
        b_row=rowg[HB+h:HB+h+1,:]
        S0f=s0_ref[0,:,sl].astype(f32)
        dSf=dS[:,sl]
        dSS=jnp.sum(dSf*S0f,axis=0,keepdims=True)*jnp.exp(cl)
        dS[:,sl]=jnp.exp(cl)*dSf+tn(Yb[h],Z[h])
        dM=dAM[h][0:C]; dA=dAM[h][C:3*C]
        xm=dM*Eq[h]; xa=dA*EA[h]
        XM=xm*GP[h][0:C]; XA=xa*GP[h][C:3*C]
        cs=jnp.sum(XM,axis=0,keepdims=True)+jnp.sum(XA,axis=0,keepdims=True)
        rows.append((cs,b_row*cs,dSS))
        XMb=XM*b_row
        XAb=XA*b_row
        rs=jnp.sum(XMb+XAb[0:C]+XAb[C:2*C],axis=-1,keepdims=True)
        yz=Y[h]*ZS[h]
        rs=rs+jnp.sum(yz[0:C]+yz[C:2*C]+yz[2*C:3*C],axis=-1,keepdims=True)
        ku=K[h]*UdS[h]
        d0=ews[h]*jnp.sum(ku[0:C],axis=-1,keepdims=True)
        d1=ews[h]*jnp.sum(ku[C:2*C],axis=-1,keepdims=True)
        colout=jnp.where(lane==h,rs,colout)
        colout=jnp.where(lane==HB+h,d0,colout)
        colout=jnp.where(lane==2*HB+h,d1,colout)
        X.append(lo(cat(xm*b_row,xa[0:C]*b_row,xa[C:2*C]*b_row)))
    col_ref[...]=colout
    row_ref[0]=jnp.concatenate([rows[h][i] for i in range(3) for h in H]+[jnp.zeros((16-3*HB,128),f32)],axis=0)
    XK=[nn(X[h],Kb[h]) for h in H]
    XY=[tn(X[h],Yb[h]) for h in H]
    def l2b(g,nrm,r):
        return r*(g-nrm*jnp.sum(g*nrm,axis=-1,keepdims=True))
    for h in H:
        ew=ews[h]
        w0=ew*colg[:,HB+h:HB+h+1]
        w1=ew*colg[:,2*HB+h:2*HB+h+1]
        sl=lambda s: slice(s*W+h*128,s*W+h*128+128)
        dq=ZS[h][0:C]+XK[h][0:C]
        dk=ZS[h][C:3*C]+XK[h][C:3*C]+XY[h]
        dk0=dk[0:C]+w0*UdS[h][0:C]
        dk1=dk[C:2*C]+w1*UdS[h][C:2*C]
        gs[0:C,sl(0)]=l2b(dq*(128**-0.5),Q[h]*(128**0.5),rq[h])*dq_s[h]
        gs[0:C,sl(1)]=l2b(dk0,K[h][0:C],rk0[h])*dk0_s[h]
        gs[0:C,sl(2)]=l2b(dk1,K[h][C:2*C],rk1[h])*dk1_s[h]
        for j in range(2):
            y=conv(3+j,h); sg=sigmoid(y)
            gs[0:C,sl(3+j)]=dR[h][j*C:j*C+C]*(sg*(1.0+y*(1.0-sg)))
        for s in range(5):
            g=gs[0:C,sl(s)]
            gx=cw_ref[3:4,sl(s)]*g
            dcw_ref[3,:,sl(s)]+=jnp.sum((g*xs[8:8+C,sl(s)]).reshape(C//8,8,128),axis=0)
            for i in range(3):
                gx=gx+cw_ref[i:i+1,sl(s)]*gs[3-i:3-i+C,sl(s)]
                dcw_ref[i,:,sl(s)]+=jnp.sum((g*xs[5+i:5+i+C,sl(s)]).reshape(C//8,8,128),axis=0)
            gx_ref[:,sl(s)]=lo(gx)

def mixer_bwd(x,cw,colg,rowg,nh,gm,o,s0,t,u,nseq):
    C=BLOCK
    R=x.shape[0]; nch=R//nseq//C; W=HB*128; ng=GROUPS
    ch=lambda s,n: s*nch+nch-1-n
    rb=lambda g,s,n:(ch(s,n),g)
    cb=lambda g,s,n:(ch(s,n),0,g)
    NC=nseq*nch
    return pl.pallas_call(
        functools.partial(bwd_body,C,HB),
        grid=(ng,nseq,nch),
        in_specs=[pl.BlockSpec((C,6*W),rb),
                  pl.BlockSpec((8,6*W),lambda g,s,n:(jnp.maximum(ch(s,n)*(C//8)-1,0),g)),
                  pl.BlockSpec((4,5*W),lambda g,s,n:(0,g)),
                  pl.BlockSpec((C,128),rb),pl.BlockSpec((1,2*HB,128),lambda g,s,n:(ch(s,n),g,0)),
                  pl.BlockSpec((1,128),lambda g,s,n:(0,0)),
                  pl.BlockSpec((C,W),rb),pl.BlockSpec((C,W),rb),
                  pl.BlockSpec((1,128,W),cb),pl.BlockSpec((1,128,W),cb),pl.BlockSpec((1,128,W),cb)],
        out_specs=[pl.BlockSpec((C,6*W),rb),pl.BlockSpec((C,128),rb),
                   pl.BlockSpec((1,16,128),lambda g,s,n:(ch(s,n),g,0)),
                   pl.BlockSpec((4,8,5*W),lambda g,s,n:(0,0,g)),
                   pl.BlockSpec((1,8,128),lambda g,s,n:(g,0,0))],
        out_shape=[jax.ShapeDtypeStruct((R,ng*6*W),bf16),jax.ShapeDtypeStruct((R,ng*128),f32),
                   jax.ShapeDtypeStruct((NC,ng*16,128),f32),
                   jax.ShapeDtypeStruct((4,8,ng*5*W),f32),jax.ShapeDtypeStruct((ng,8,128),f32)],
        scratch_shapes=[pltpu.VMEM((C+8,5*W),f32),pltpu.VMEM((C+8,5*W),f32),pltpu.VMEM((128,W),f32)],
        compiler_params=pltpu.CompilerParams(dimension_semantics=("arbitrary",)*3,vmem_limit_bytes=48<<20),
        name="mixer_bwd",
    )(x,x,cw,colg,rowg,nh,gm,o,s0,t,u)

def make_gates(small,a_log,dt_bias):
    C=BLOCK
    R=small.shape[0]; NC=R//C; ng=8//HB
    beta=jax.nn.sigmoid(small[:,:16])
    pre=small[:,16:24]+dt_bias
    g=-jnp.exp(a_log)*jax.nn.softplus(pre)
    c=jnp.cumsum(g.reshape(NC,C,8),axis=1)
    cf=c.reshape(R,8)
    gr=lambda z: z.reshape(R,ng,HB)
    colg=jnp.concatenate([gr(cf),gr(beta[:,:8]),gr(beta[:,8:]),jnp.zeros((R,ng,128-3*HB),f32)],axis=2).reshape(R,ng*128)
    ct=c.transpose(0,2,1)
    crow=jnp.concatenate([ct,ct],axis=2).reshape(NC,ng,HB,2*C)
    b=beta.reshape(NC,C,2,8).transpose(0,3,2,1).reshape(NC,ng,HB,2*C)
    rowg=jnp.concatenate([crow,b],axis=2).reshape(NC,ng*2*HB,2*C)
    return colg,rowg,(beta,pre,g)

def gates_bwd(col,row,saved,a_log):
    C=BLOCK
    beta,pre,g=saved
    R=beta.shape[0]; NC=R//C; ng=8//HB
    co=col.reshape(R,ng,128)
    rs=co[:,:,:HB].reshape(NC,C,8)
    d0=co[:,:,HB:2*HB].reshape(R,8); d1=co[:,:,2*HB:3*HB].reshape(R,8)
    ro=row.reshape(NC,ng,16,128)
    tr=lambda z: z.reshape(NC,8,2,C).transpose(0,3,2,1)
    cs=tr(ro[:,:,:HB]); csb=tr(ro[:,:,HB:2*HB]); dss=jnp.sum(ro[:,:,2*HB:3*HB],axis=-1).reshape(NC,8)
    dw=jnp.stack([d0,d1],axis=1)
    dbeta=cs.reshape(R,2,8)+dw
    bdw=(beta.reshape(R,2,8)*dw).reshape(NC,C,2,8)
    dc=rs-jnp.sum(csb+bdw,axis=2)
    dcl=dss+jnp.sum(bdw,axis=(1,2))
    dg=lax.cumsum(dc,axis=1,reverse=True)+dcl[:,None,:]
    dg=dg.reshape(R,8)
    dbeta=dbeta.reshape(R,16)
    dsmall_b=dbeta*beta*(1.0-beta)
    dpre=dg*(-jnp.exp(a_log))*jax.nn.sigmoid(pre)
    g_alog=jnp.sum(dg*g,axis=0)
    g_dtb=jnp.sum(dpre,axis=0)
    return jnp.concatenate([dsmall_b,dpre],axis=1),g_alog,g_dtb


def to_groups(w):
    rows = w.shape[0]
    return w.reshape(rows, 6, GROUPS, HB * DK).transpose(0, 2, 1, 3).reshape(rows, w.shape[1])


def from_groups(w):
    rows = w.shape[0]
    return w.reshape(rows, GROUPS, 6, HB * DK).transpose(0, 2, 1, 3).reshape(rows, w.shape[1])


def all_sum(vec, total):
    axes = ("rep", "shard")
    step = 1
    while step < total:
        vec = vec + lax.ppermute(vec, axes, [(i, i ^ step) for i in range(total)])
        step *= 2
    return vec


def gather(w):
    return lax.all_gather(w, "shard", axis=0, tiled=True)


def scatter(w):
    return lax.psum_scatter(w, "shard", scatter_dimension=0, tiled=True)


def shards(
    total,
    hidden_in,
    teacher,
    cotangent,
    lengths,
    norm_attn,
    w_in,
    w_small,
    conv_w,
    a_log,
    dt_bias,
    norm_head,
    w_out,
    norm_mlp,
    w_mlp_in,
    w_mlp_down,
):
    row_count, width = hidden_in.shape
    seq_here = lengths.shape[0]
    slot_count = row_count // seq_here
    small_width = w_small.shape[1]
    proj_width = w_in.shape[1]
    wide = jnp.concatenate(
        [to_groups(w_in), jnp.pad(w_small, ((0, 0), (0, 128 - small_width)))], axis=1
    )
    wide_all = gather(wide)
    w_out_all = gather(w_out)
    w_mlp_in_all = gather(w_mlp_in)
    w_down_all = gather(w_mlp_down)

    hidden32 = hidden_in.astype(f32)
    r_in = lax.rsqrt(jnp.mean(hidden32 * hidden32, axis=-1, keepdims=True) + EPSILON)
    normed_low = (hidden32 * r_in * norm_attn).astype(bf16)
    proj = dot_plain(normed_low, wide_all)
    small = proj[:, proj_width : proj_width + small_width]
    conv_pad = jnp.pad(conv_w, ((0, 0), (0, proj_width - conv_w.shape[1])))
    conv_groups = to_groups(conv_pad).reshape(4, GROUPS, 6 * HB * DK)[:, :, : 5 * HB * DK]
    conv_groups = conv_groups.reshape(4, GROUPS * 5 * HB * DK)
    head_gain = norm_head.reshape(1, DK)
    colg, rowg, saved = make_gates(small, a_log, dt_bias)
    mixed_low, heads_out, states, inverses, updates = mixer_fwd(
        proj, conv_groups, colg, rowg, head_gain, seq_here
    )
    residual = hidden32 + dot_plain(mixed_low, w_out_all)
    r_mid = lax.rsqrt(jnp.mean(residual * residual, axis=-1, keepdims=True) + EPSILON)
    mid_low = (residual * r_mid * norm_mlp).astype(bf16)
    gate_up = dot_plain(mid_low, w_mlp_in_all)
    unit_count = w_down_all.shape[0]
    gate_part = gate_up[:, :unit_count]
    up_part = gate_up[:, unit_count:]
    sigmoid_gate = jax.nn.sigmoid(gate_part)
    silu_gate = gate_part * sigmoid_gate
    product_low = (silu_gate * up_part).astype(bf16)
    output32 = residual + dot_plain(product_low, w_down_all)
    slot_index = lax.broadcasted_iota(jnp.int32, (seq_here, slot_count), 1)
    valid_rows = (slot_index < lengths[:, None]).astype(f32).reshape(row_count, 1)
    deviation = output32 - teacher.astype(f32)
    loss_sum = jnp.sum(valid_rows * deviation * deviation)
    valid_count = jnp.sum(lengths).astype(f32)
    grad_out = valid_rows * (cotangent.astype(f32) + deviation)
    grad_out_low = grad_out.astype(bf16)

    grad_w_down = dot_left_t(product_low, grad_out_low).astype(bf16)
    own_down = scatter(grad_w_down)
    grad_product = dot_right_t(grad_out_low, w_down_all)
    grad_gate = grad_product * up_part * sigmoid_gate * (1.0 + gate_part * (1.0 - sigmoid_gate))
    grad_up = grad_product * silu_gate
    grad_gate_up = jnp.concatenate([grad_gate, grad_up], axis=1).astype(bf16)
    grad_w_mlp_in = dot_left_t(mid_low, grad_gate_up).astype(bf16)
    own_mlp_in = scatter(grad_w_mlp_in)
    grad_mid = dot_right_t(grad_gate_up, w_mlp_in_all)
    u_mid = grad_mid * norm_mlp
    grad_norm_mlp = jnp.sum(grad_mid * residual * r_mid, axis=0)
    grad_residual = (
        grad_out
        + r_mid * u_mid
        - (r_mid * r_mid * r_mid) * residual * jnp.mean(u_mid * residual, axis=-1, keepdims=True)
    )
    grad_res_low = grad_residual.astype(bf16)
    grad_mixed = dot_right_t(grad_res_low, w_out_all)
    grad_w_out = dot_left_t(mixed_low, grad_res_low).astype(bf16)
    own_out = scatter(grad_w_out)
    own_down, own_mlp_in, own_out = lax.psum((own_down, own_mlp_in, own_out), "rep")

    grad_proj_low, col_out, row_out, conv_out, gain_out = mixer_bwd(
        proj, conv_groups, colg, rowg, head_gain, grad_mixed, heads_out, states, inverses,
        updates, seq_here,
    )
    grad_small, grad_log, grad_bias = gates_bwd(col_out, row_out, saved, a_log)
    grad_small_low = jnp.pad(grad_small.astype(bf16), ((0, 0), (0, 128 - small_width)))
    grad_wide = jnp.concatenate(
        [dot_left_t(normed_low, grad_proj_low), dot_left_t(normed_low, grad_small_low)], axis=1
    ).astype(bf16)
    own_wide = scatter(grad_wide)
    own_wide, own_down, own_mlp_in, own_out = lax.optimization_barrier(
        (own_wide, own_down, own_mlp_in, own_out)
    )
    own_wide = lax.psum(own_wide, "rep").astype(f32)
    grad_normed = dot_right_t(grad_proj_low, wide_all[:, :proj_width]) + dot_right_t(
        grad_small_low, wide_all[:, proj_width:]
    )
    u_in = grad_normed * norm_attn
    grad_norm_attn = jnp.sum(grad_normed * hidden32 * r_in, axis=0)
    grad_hidden = (
        grad_residual
        + r_in * u_in
        - (r_in * r_in * r_in) * hidden32 * jnp.mean(u_in * hidden32, axis=-1, keepdims=True)
    ).astype(bf16)

    grad_conv = jnp.sum(conv_out, axis=1).reshape(4, GROUPS, 5, HB * DK)
    grad_conv = grad_conv.transpose(0, 2, 1, 3).reshape(4, conv_w.shape[1])
    grad_gain = jnp.sum(gain_out, axis=(0, 1))
    parts = (
        grad_norm_attn,
        grad_conv.reshape(-1),
        grad_norm_mlp,
        grad_gain,
        grad_log,
        grad_bias,
        loss_sum.reshape(1),
        valid_count.reshape(1),
        jnp.zeros((110,), f32),
    )
    packed = jnp.concatenate(parts).reshape(-1, 128)
    packed = all_sum(packed, total).reshape(-1)
    sums = []
    start = 0
    for part in parts:
        sums.append(packed[start : start + part.shape[0]])
        start += part.shape[0]
    loss_value = sums[6][0] / (sums[7][0] * width)
    return (
        output32.astype(bf16),
        loss_value,
        grad_hidden,
        sums[0],
        from_groups(own_wide[:, :proj_width]),
        own_wide[:, proj_width : proj_width + small_width],
        sums[1].reshape(conv_w.shape),
        sums[4],
        sums[5],
        sums[3],
        own_out.astype(f32),
        sums[2],
        own_mlp_in.astype(f32),
        own_down.astype(f32),
    )


def solution(mesh):
    total = mesh.shape["rep"] * mesh.shape["shard"]
    in_specs = (
        P(("rep", "shard"), None),
        P(("rep", "shard"), None),
        P(("rep", "shard"), None),
        P(("rep", "shard")),
        P(),
        P("shard", None),
        P("shard", None),
        P(),
        P(),
        P(),
        P(),
        P("shard", None),
        P(),
        P("shard", None),
        P("shard", None),
    )
    out_specs = (
        P(("rep", "shard"), None),
        P(),
        P(("rep", "shard"), None),
        P(),
        P("shard", None),
        P("shard", None),
        P(),
        P(),
        P(),
        P(),
        P("shard", None),
        P(),
        P("shard", None),
        P("shard", None),
    )
    return jax.shard_map(
        functools.partial(shards, total),
        mesh=mesh,
        in_specs=in_specs,
        out_specs=out_specs,
        check_vma=False,
    )
```

```python
import functools

import jax
import jax.numpy as jnp
from jax import lax
from jax.experimental import pallas as pl
from jax.experimental.pallas import tpu as pltpu
from jax.sharding import PartitionSpec as P

HEADS = 8
DK = 128
HOUSE = 2
BLOCK = 64
EPSILON = 1e-06
EPS = EPSILON
f32 = jnp.float32
bf16 = jnp.bfloat16


def dot_plain(a,b): return nn(a,b)
def dot_right_t(a,b): return nt(a,b)
def dot_left_t(a,b): return tn(a,b)
def nn(a,b): return lax.dot_general(a,b,(((1,),(0,)),((),())),preferred_element_type=f32)
def nt(a,b): return lax.dot_general(a,b,(((1,),(1,)),((),())),preferred_element_type=f32)
def tn(a,b): return lax.dot_general(a,b,(((0,),(0,)),((),())),preferred_element_type=f32)
def lo(x): return x.astype(bf16)
def sigmoid(x): return 0.5*jnp.tanh(0.5*x)+0.5
def cat(*xs): return jnp.concatenate(xs,axis=0)

def token_masks(C):
    row=lax.broadcasted_iota(jnp.int32,(C,2*C),0)
    col=lax.broadcasted_iota(jnp.int32,(C,2*C),1)
    left=col<C
    tok=jnp.where(left,col,col-C)
    return row,tok,left

LU=2
PREC=lax.Precision.HIGHEST

def exact(a,b,dims): return lax.dot_general(a,b,(dims,((),())),precision=PREC,preferred_element_type=f32)

def col6(slot,h):
    at=(h//LU)*6*LU*128+slot*LU*128+(h%LU)*128
    return slice(at,at+128)

def col5(slot,h):
    at=(h//LU)*5*LU*128+slot*LU*128+(h%LU)*128
    return slice(at,at+128)

def coln(slot,h):
    at=slot*HEADS*DK+h*DK
    return slice(at,at+DK)

def gates(colg,rowg,h):
    return colg[:,16+h:17+h],rowg[8+h:9+h,:],rowg[h:h+1,:]

def softplus(v): return jnp.maximum(v,0.0)+jnp.log1p(jnp.exp(-jnp.abs(v)))

def eyes(C):
    row,tok,left=token_masks(C)
    here=tok==row
    return jnp.where(here&left,1.0,0.0),jnp.where(here&jnp.logical_not(left),1.0,0.0),jnp.where(row<=tok,1.0,0.0)

def square_mask(C,upper):
    a=lax.broadcasted_iota(jnp.int32,(C,C),0)
    b=lax.broadcasted_iota(jnp.int32,(C,C),1)
    return jnp.where((b>=a) if upper else (b<=a),1.0,0.0)

def gate_body(C,NB,sm_ref,par_ref,col_ref,row_ref):
    eyeL,eyeR,tri2=eyes(C)
    tri=square_mask(C,False)
    lane=lax.broadcasted_iota(jnp.int32,(C,128),1)
    for b in range(NB):
        sl=slice(b*C,b*C+C)
        sm=sm_ref[sl,:]
        beta=sigmoid(sm)
        g=par_ref[0:1,:]*softplus(sm+par_ref[1:2,:])
        c=exact(tri,g,((1,),(0,)))
        col_ref[sl,:]=jnp.where(lane<16,beta,c)
        crow=exact(g,tri2,((0,),(0,)))
        brow=exact(beta,eyeL,((0,),(0,)))[0:8]+exact(beta,eyeR,((0,),(0,)))[8:16]
        row_ref[b,0:8,:]=brow
        row_ref[b,8:16,:]=crow[16:24]

def gate_fwd(small,par,C,NB=4,at=0):
    R=small.shape[0]; NC=R//C
    return pl.pallas_call(
        functools.partial(gate_body,C,NB),grid=(NC//NB,),
        in_specs=[pl.BlockSpec((NB*C,128),lambda n:(n,at)),pl.BlockSpec((8,128),lambda n:(0,0))],
        out_specs=[pl.BlockSpec((NB*C,128),lambda n:(n,0)),pl.BlockSpec((NB,16,128),lambda n:(n,0,0))],
        out_shape=[jax.ShapeDtypeStruct((R,128),f32),jax.ShapeDtypeStruct((NC,16,128),f32)],
        name="gate_fwd")(small,par)

def gate_bwd_body(C,NB,K,*refs):
    sm_ref,par_ref,colg_ref=refs[:3]
    cols=refs[3:3+K]; rows=refs[3+K:3+2*K]
    out_ref,acc_ref=refs[3+2*K:]
    @pl.when(pl.program_id(0)==0)
    def _():
        acc_ref[...]=jnp.zeros_like(acc_ref)
    eyeL,eyeR,tri2=eyes(C)
    tru=square_mask(C,True)
    lane=lax.broadcasted_iota(jnp.int32,(C,128),1)
    z=lambda n: jnp.zeros((n,128),f32)
    part=lambda v: jnp.sum(v.reshape(C//8,8,128),axis=0)
    for b in range(NB):
        sl=slice(b*C,b*C+C)
        col=cols[0][sl,:]; row=rows[0][b]
        for k in range(1,K):
            col=col+cols[k][sl,:]; row=row+rows[k][b]
        cs=row[0:8]; dss=row[8:16]
        ccs=exact(eyeL,cat(cs,z(120)),((1,),(1,)))+exact(eyeR,cat(z(8),cs,z(112)),((1,),(1,)))
        beta=jnp.where(lane<16,colg_ref[sl,:],0.0)
        d=jnp.where(lane<16,col,0.0)
        dbeta=ccs+d
        y=beta*dbeta
        dc=col-pltpu.roll(y,16,1)-pltpu.roll(y,8,1)
        bd=jnp.sum(beta*d,axis=0,keepdims=True)
        bd=cat(bd,z(7))
        dcl=exact(jnp.ones((8,128),f32),cat(z(16),dss,z(104)),((1,),(1,)))[0:1]+(pltpu.roll(bd,16,1)+pltpu.roll(bd,8,1))[0:1]
        keep=(lane>=16)&(lane<24)
        dc=jnp.where(keep,dc,0.0)
        dg=exact(tru,dc,((1,),(0,)))+dcl
        dg=jnp.where(keep,dg,0.0)
        pre=sm_ref[sl,:]+par_ref[1:2,:]
        g=par_ref[0:1,:]*softplus(pre)
        dpre=dg*par_ref[0:1,:]*sigmoid(pre)
        out_ref[sl,:]=lo(jnp.where(lane<16,dbeta*beta*(1.0-beta),dpre))
        acc_ref[0:8,:]+=part(dpre)
        acc_ref[8:16,:]+=part(dg*g)

def gate_bwd(small,par,colg,cols,rows,C,NB=4,at=0):
    R=small.shape[0]; NC=R//C; K=len(cols)
    cspec=pl.BlockSpec((NB*C,128),lambda n:(n,0)); rspec=pl.BlockSpec((NB,16,128),lambda n:(n,0,0))
    return pl.pallas_call(
        functools.partial(gate_bwd_body,C,NB,K),grid=(NC//NB,),
        in_specs=[pl.BlockSpec((NB*C,128),lambda n:(n,at)),pl.BlockSpec((8,128),lambda n:(0,0)),cspec]+[cspec]*K+[rspec]*K,
        out_specs=[cspec,pl.BlockSpec((16,128),lambda n:(0,0))],
        out_shape=[jax.ShapeDtypeStruct((R,128),bf16),jax.ShapeDtypeStruct((16,128),f32)],
        name="gate_bwd")(small,par,colg,*cols,*rows)

def fwd_body(C,HB,NB,hoff,x_ref,cw_ref,colg_ref,rowg_ref,nh_ref,*refs):
    mixed_ref,o_ref,s0_ref,t_ref,u_ref,xs,S=refs[-7:]
    fwd_main(C,HB,NB,hoff,x_ref,cw_ref,colg_ref,rowg_ref,nh_ref,mixed_ref,o_ref,s0_ref,t_ref,u_ref,xs,S)

def fwd_main(C,HB,NB,hoff,x_ref,cw_ref,colg_ref,rowg_ref,nh_ref,mixed_ref,o_ref,s0_ref,t_ref,u_ref,xs,S):
    NR=NB*C
    nu=HB//LU
    @pl.when(pl.program_id(1)==0)
    def _():
        xs[0:8,:]=jnp.zeros((8,xs.shape[1]),f32)
        S[...]=jnp.zeros_like(S)
    @pl.when(pl.program_id(1)!=0)
    def _():
        xs[0:8,:]=xs[NR:NR+8,:]
    for u in range(nu):
        w5=5*LU*128
        xs[8:8+NR,u*w5:(u+1)*w5]=x_ref[:,u*6*LU*128:u*6*LU*128+w5].astype(f32)
    row,tok,left=token_masks(C)
    incl=tok<=row
    strict=tok<row
    botm=tok<row+jnp.where(left,1,0)
    eye=jnp.where((tok==row)&left,1.0,0.0)
    eye2=jnp.where((tok==row)&jnp.logical_not(left),1.0,0.0)
    def act(slot,b,h):
        sl=col5(slot,h)
        cn=coln(slot,hoff+h)
        y=cw_ref[3:4,cn]*xs[8+b*C:8+b*C+C,sl]
        for i in range(3):
            y=y+cw_ref[i:i+1,cn]*xs[5+i+b*C:5+i+b*C+C,sl]
        return y*sigmoid(y)
    def l2(a): return a*lax.rsqrt(jnp.sum(a*a,axis=-1,keepdims=True)+EPS)
    H=[(b,h) for b in range(NB) for h in range(HB)]
    colg=[colg_ref[b*C:b*C+C,:] for b in range(NB)]
    rowg=[rowg_ref[b] for b in range(NB)]
    Q={};K={};V={};Y={};Kb={};GP={};A={};M={};T={}
    for p in H:
        b,h=p
        Q[p]=l2(act(0,b,h))*(128**-0.5)
        K[p]=cat(l2(act(1,b,h)),l2(act(2,b,h)))
        V[p]=cat(act(3,b,h),act(4,b,h))
        Y[p]=lo(cat(Q[p],K[p]))
        Kb[p]=lo(K[p])
    for p in H:
        GP[p]=nt(Y[p],Kb[p])
    for p in H:
        b,h=p
        c_col,c_row,b_row=gates(colg[b],rowg[b],hoff+h)
        e=jnp.exp(jnp.minimum(c_col-c_row,0.0))*b_row
        M[p]=lo(jnp.where(incl,GP[p][0:C]*e,0.0))
        A[p]=cat(jnp.where(strict,GP[p][C:2*C]*e,0.0),jnp.where(botm,GP[p][2*C:3*C]*e,0.0))
        T[p]=cat(eye,eye2-A[p][C:2*C]*eye)
    s=1
    while s<C:
        m=((tok//(2*s))==(row//(2*s)))&((row//s)%2==1)&((tok//s)%2==0)
        mf=jnp.where(m,1.0,0.0)
        Tb={p:lo(T[p]) for p in H}
        Z={p:nn(lo(cat(A[p][0:C]*mf,A[p][C:2*C]*mf)),Tb[p]) for p in H}
        T={p:T[p]-nn(Tb[p],lo(Z[p])) for p in H}
        s*=2
    Tb={p:lo(T[p]) for p in H}
    for b in range(NB):
        S0=[S[:,h*128:h*128+128] for h in range(HB)]
        S0b=[lo(v) for v in S0]
        YS=[nn(Y[b,h],S0b[h]) for h in range(HB)]
        U=[]
        for h in range(HB):
            ec=jnp.exp(colg[b][:,16+hoff+h:17+hoff+h])
            ks=YS[h][C:3*C]
            R=V[b,h]-cat(ec*ks[0:C],ec*ks[C:2*C])
            U.append(lo(nn(Tb[b,h],lo(R))))
        for h in range(HB):
            sl=slice(h*128,h*128+128)
            G=hoff+h
            rows=slice(b*C,b*C+C)
            c_col=colg[b][:,16+G:17+G]
            ec=jnp.exp(c_col)
            cl=c_col[C-1:C]
            ew=jnp.exp(cl-c_col)
            w0=ew*colg[b][:,G:G+1]
            w1=ew*colg[b][:,8+G:9+G]
            kw=lo(cat(w0*K[b,h][0:C],w1*K[b,h][C:2*C]))
            S[:,sl]=jnp.exp(cl)*S0[h]+tn(kw,U[h])
            O=ec*YS[h][0:C]+nn(M[b,h],U[h])
            s0_ref[b,:,sl]=S0b[h]
            t_ref[b,:,sl]=Tb[b,h]
            u_ref[b,:,sl]=U[h]
            o_ref[rows,sl]=O
            g=x_ref[rows,col6(5,h)].astype(f32)
            r=lax.rsqrt(jnp.mean(O*O,axis=-1,keepdims=True)+EPS)
            mixed_ref[rows,sl]=lo(O*r*nh_ref[...]*(g*sigmoid(g)))

def mixer_fwd(x,cw,colg,rowg,nh,nseq,hoff,HB,C,NB=2,mixed=None):
    R=x.shape[0]; nch=R//nseq//C//NB; W=HB*128
    rb=lambda s,n:(s*nch+n,0)
    cb=lambda s,n:(s*nch+n,0,0)
    NC=R//C
    big=pl.BlockSpec((NB,128,W),cb)
    state=jax.ShapeDtypeStruct((NC,128,W),bf16)
    return pl.pallas_call(
        functools.partial(fwd_body,C,HB,NB,hoff),
        grid=(nseq,nch),
        in_specs=[pl.BlockSpec((NB*C,6*W),rb),pl.BlockSpec((4,5*HEADS*DK),lambda s,n:(0,0)),
                  pl.BlockSpec((NB*C,128),rb),pl.BlockSpec((NB,16,128),cb),
                  pl.BlockSpec((1,128),lambda s,n:(0,0))]+([pl.BlockSpec(memory_space=pl.ANY)] if mixed is not None else []),
        input_output_aliases={5:0} if mixed is not None else {},
        out_specs=[pl.BlockSpec((NB*C,W),lambda s,n:(s*nch+n,hoff//HB)),pl.BlockSpec((NB*C,W),rb),big,big,big],
        out_shape=[jax.ShapeDtypeStruct((R,HEADS*DK),bf16),jax.ShapeDtypeStruct((R,W),f32),state,state,state],
        scratch_shapes=[pltpu.VMEM((NB*C+8,5*W),f32),pltpu.VMEM((128,W),f32)],
        compiler_params=pltpu.CompilerParams(dimension_semantics=("arbitrary",)*2,vmem_limit_bytes=56<<20),
        cost_estimate=pl.CostEstimate(flops=HB*10_000_000_000,transcendentals=0,bytes_accessed=HB*30_000_000),
        name="mixer_fwd",
    )(x,cw,colg,rowg,nh,*(() if mixed is None else (mixed,)))

def bwd_body(C,HB,hoff,x_ref,xp_ref,cw_ref,colg_ref,rowg_ref,nh_ref,gm_ref,o_ref,s0_ref,t_ref,u_ref,
             gx_ref,col_ref,row_ref,dcw_ref,dnh_ref,xs,gs,dS):
    W=HB*128
    CV=5*W
    n=pl.program_id(1); nch=pl.num_programs(1)
    first=(pl.program_id(0)==0)&(n==0)
    @pl.when(first)
    def _():
        dcw_ref[...]=jnp.zeros_like(dcw_ref)
        dnh_ref[...]=jnp.zeros_like(dnh_ref)
    @pl.when(n==0)
    def _():
        gs[C:C+8,:]=jnp.zeros((8,CV),f32)
        dS[...]=jnp.zeros_like(dS)
    @pl.when(n!=0)
    def _():
        gs[C:C+8,:]=gs[0:8,:]
    @pl.when(n==nch-1)
    def _():
        xs[0:8,:]=jnp.zeros((8,CV),f32)
    w5=5*LU*128
    parts=[(slice(u*w5,(u+1)*w5),slice(u*6*LU*128,u*6*LU*128+w5)) for u in range(HB//LU)]
    @pl.when(n!=nch-1)
    def _():
        for to,at in parts:
            xs[0:8,to]=xp_ref[:,at].astype(f32)
    for to,at in parts:
        xs[8:8+C,to]=x_ref[:,at].astype(f32)
    row,tok,left=token_masks(C)
    incl=tok<=row
    strict=tok<row
    botm=tok<row+jnp.where(left,1,0)
    colg=colg_ref[...]
    rowg=rowg_ref[0]
    lane=lax.broadcasted_iota(jnp.int32,(C,128),1)
    H=range(HB)
    def conv(slot,h):
        sl=col5(slot,h)
        cn=coln(slot,hoff+h)
        y=cw_ref[3:4,cn]*xs[8:8+C,sl]
        for i in range(3):
            y=y+cw_ref[i:i+1,cn]*xs[5+i:5+i+C,sl]
        return y
    def act_norm(slot,h):
        y=conv(slot,h)
        sg=sigmoid(y)
        a=y*sg
        r=lax.rsqrt(jnp.sum(a*a,axis=-1,keepdims=True)+EPS)
        dsil=sg*(1.0+y*(1.0-sg))
        return a*r,r,dsil
    Q=[];K=[];rq=[];rk0=[];rk1=[];dq_s=[];dk0_s=[];dk1_s=[]
    for h in H:
        a,r,d=act_norm(0,h); Q.append(a*(128**-0.5)); rq.append(r); dq_s.append(d)
        a0,r0,d0=act_norm(1,h); a1,r1,d1=act_norm(2,h)
        K.append(cat(a0,a1)); rk0.append(r0); rk1.append(r1); dk0_s.append(d0); dk1_s.append(d1)
    dO=[]
    nhg=nh_ref[...]
    for h in H:
        sl=slice(h*128,h*128+128)
        O=o_ref[:,sl]; gm=gm_ref[:,sl].astype(f32)
        gt=x_ref[:,col6(5,h)].astype(f32)
        sg=sigmoid(gt)
        r=lax.rsqrt(jnp.mean(O*O,axis=-1,keepdims=True)+EPS)
        on=O*r
        gsil=gm*(gt*sg)
        t1=gsil*on
        dnh_ref[0]+=jnp.sum(t1.reshape(C//8,8,128),axis=0)
        dgt=gm*(on*nhg)*(sg*(1.0+gt*(1.0-sg)))
        gx_ref[:,col6(5,h)]=lo(dgt)
        u=gsil*nhg
        dO.append(r*(u-on*jnp.mean(u*on,axis=-1,keepdims=True)))
    Y=[cat(Q[h],K[h]) for h in H]
    Yb=[lo(y) for y in Y]
    Kb=[lo(K[h]) for h in H]
    GP=[nt(Yb[h],Kb[h]) for h in H]
    dU=[];Eq=[];EA=[];dSb=[];ecs=[];ews=[]
    for h in H:
        sl=slice(h*128,h*128+128)
        c_col,c_row,b_row=gates(colg,rowg,hoff+h)
        e=jnp.exp(jnp.minimum(c_col-c_row,0.0))
        eq=jnp.where(incl,e,0.0); ea=cat(jnp.where(strict,e,0.0),jnp.where(botm,e,0.0))
        Eq.append(eq);EA.append(ea)
        M=lo(GP[h][0:C]*eq*b_row)
        cl=colg[C-1:C,16+hoff+h:17+hoff+h]
        ec=jnp.exp(c_col); ew=jnp.exp(cl-c_col)
        ecs.append(ec);ews.append(ew)
        w0=ew*colg[:,hoff+h:hoff+h+1]
        w1=ew*colg[:,8+hoff+h:9+hoff+h]
        kw=lo(cat(w0*K[h][0:C],w1*K[h][C:2*C]))
        db_=lo(dS[:,sl]); dSb.append(db_)
        dU.append(lo(tn(M,lo(dO[h]))+nn(kw,db_)))
    dR=[tn(t_ref[0,:,h*128:h*128+128],dU[h]) for h in H]
    dAM=[nt(lo(cat(dO[h],-dR[h])),u_ref[0,:,h*128:h*128+128]) for h in H]
    Z=[]
    for h in H:
        ec=ecs[h]
        Z.append(lo(cat(ec*dO[h],-(ec*dR[h][0:C]),-(ec*dR[h][C:2*C]))))
    UdS=[nt(u_ref[0,:,h*128:h*128+128],dSb[h]) for h in H]
    colout=jnp.zeros((C,128),f32)
    rows=[]
    X=[]
    ZS=[nt(Z[h],s0_ref[0,:,h*128:h*128+128]) for h in H]
    for h in H:
        sl=slice(h*128,h*128+128)
        cl=colg[C-1:C,16+hoff+h:17+hoff+h]
        b_row=rowg[hoff+h:hoff+h+1,:]
        S0f=s0_ref[0,:,sl].astype(f32)
        dSf=dS[:,sl]
        dSS=jnp.sum(dSf*S0f,axis=0,keepdims=True)*jnp.exp(cl)
        dS[:,sl]=jnp.exp(cl)*dSf+tn(Yb[h],Z[h])
        dM=dAM[h][0:C]; dA=dAM[h][C:3*C]
        xm=dM*Eq[h]; xa=dA*EA[h]
        XM=xm*GP[h][0:C]; XA=xa*GP[h][C:3*C]
        cs=jnp.sum(XM,axis=0,keepdims=True)+jnp.sum(XA,axis=0,keepdims=True)
        rows.append((cs,dSS))
        XMb=XM*b_row
        XAb=XA*b_row
        rs=jnp.sum(XMb+XAb[0:C]+XAb[C:2*C],axis=-1,keepdims=True)
        yz=Y[h]*ZS[h]
        rs=rs+jnp.sum(yz[0:C]+yz[C:2*C]+yz[2*C:3*C],axis=-1,keepdims=True)
        ku=K[h]*UdS[h]
        d0=ews[h]*jnp.sum(ku[0:C],axis=-1,keepdims=True)
        d1=ews[h]*jnp.sum(ku[C:2*C],axis=-1,keepdims=True)
        colout=jnp.where(lane==16+hoff+h,rs,colout)
        colout=jnp.where(lane==hoff+h,d0,colout)
        colout=jnp.where(lane==8+hoff+h,d1,colout)
        X.append(lo(cat(xm*b_row,xa[0:C]*b_row,xa[C:2*C]*b_row)))
    col_ref[...]=colout
    row_ref[...]=jnp.zeros_like(row_ref)
    for h in H:
        row_ref[0,hoff+h:hoff+h+1,:]=rows[h][0]
        row_ref[0,8+hoff+h:9+hoff+h,:]=rows[h][1]
    XK=[nn(X[h],Kb[h]) for h in H]
    XY=[tn(X[h],Yb[h]) for h in H]
    def l2b(g,nrm,r):
        return r*(g-nrm*jnp.sum(g*nrm,axis=-1,keepdims=True))
    for h in H:
        ew=ews[h]
        w0=ew*colg[:,hoff+h:hoff+h+1]
        w1=ew*colg[:,8+hoff+h:9+hoff+h]
        sl=lambda s: col5(s,h)
        dq=ZS[h][0:C]+XK[h][0:C]
        dk=ZS[h][C:3*C]+XK[h][C:3*C]+XY[h]
        dk0=dk[0:C]+w0*UdS[h][0:C]
        dk1=dk[C:2*C]+w1*UdS[h][C:2*C]
        gs[0:C,sl(0)]=l2b(dq*(128**-0.5),Q[h]*(128**0.5),rq[h])*dq_s[h]
        gs[0:C,sl(1)]=l2b(dk0,K[h][0:C],rk0[h])*dk0_s[h]
        gs[0:C,sl(2)]=l2b(dk1,K[h][C:2*C],rk1[h])*dk1_s[h]
        for j in range(2):
            y=conv(3+j,h); sg=sigmoid(y)
            gs[0:C,sl(3+j)]=dR[h][j*C:j*C+C]*(sg*(1.0+y*(1.0-sg)))
        for s in range(5):
            g=gs[0:C,sl(s)]
            cn=coln(s,hoff+h)
            gx=cw_ref[3:4,cn]*g
            dcw_ref[3,:,cn]+=jnp.sum((g*xs[8:8+C,sl(s)]).reshape(C//8,8,128),axis=0)
            for i in range(3):
                gx=gx+cw_ref[i:i+1,cn]*gs[3-i:3-i+C,sl(s)]
                dcw_ref[i,:,cn]+=jnp.sum((g*xs[5+i:5+i+C,sl(s)]).reshape(C//8,8,128),axis=0)
            gx_ref[:,col6(s,h)]=lo(gx)

def mixer_bwd(x,cw,colg,rowg,nh,gm,o,s0,t,u,nseq,hoff,unit,C,HB=2):
    R=x.shape[0]; nch=R//nseq//C; W=HB*128
    ch=lambda s,n: s*nch+nch-1-n
    rb=lambda s,n:(ch(s,n),unit)
    r0=lambda s,n:(ch(s,n),0)
    cb=lambda s,n:(ch(s,n),0,unit)
    NC=nseq*nch
    big=pl.BlockSpec((1,128,W),cb)
    return pl.pallas_call(
        functools.partial(bwd_body,C,HB,hoff),
        grid=(nseq,nch),
        in_specs=[pl.BlockSpec((C,6*W),rb),
                  pl.BlockSpec((8,6*W),lambda s,n:(jnp.maximum(ch(s,n)*(C//8)-1,0),unit)),
                  pl.BlockSpec((4,5*HEADS*DK),lambda s,n:(0,0)),
                  pl.BlockSpec((C,128),r0),pl.BlockSpec((1,16,128),lambda s,n:(ch(s,n),0,0)),
                  pl.BlockSpec((1,128),lambda s,n:(0,0)),
                  pl.BlockSpec((C,W),lambda s,n:(ch(s,n),hoff//HB)),pl.BlockSpec((C,W),rb),
                  big,big,big],
        out_specs=[pl.BlockSpec((C,6*W),r0),pl.BlockSpec((C,128),r0),
                   pl.BlockSpec((1,16,128),lambda s,n:(ch(s,n),0,0)),
                   pl.BlockSpec((4,8,5*HEADS*DK),lambda s,n:(0,0,0)),
                   pl.BlockSpec((1,8,128),lambda s,n:(0,0,0))],
        out_shape=[jax.ShapeDtypeStruct((R,6*W),bf16),jax.ShapeDtypeStruct((R,128),f32),
                   jax.ShapeDtypeStruct((NC,16,128),f32),
                   jax.ShapeDtypeStruct((4,8,5*HEADS*DK),f32),jax.ShapeDtypeStruct((1,8,128),f32)],
        scratch_shapes=[pltpu.VMEM((C+8,5*W),f32),pltpu.VMEM((C+8,5*W),f32),pltpu.VMEM((128,W),f32)],
        compiler_params=pltpu.CompilerParams(dimension_semantics=("arbitrary",)*2,vmem_limit_bytes=48<<20),
        cost_estimate=pl.CostEstimate(flops=100_000_000,transcendentals=0,bytes_accessed=300_000),
        name="mixer_bwd",
    )(x,x,cw,colg,rowg,nh,gm,o,s0,t,u)


def sort_body(w_ref, small_ref, out_ref, first_ref, second_ref):
    width = LU * DK
    for unit in range(4):
        for slot in range(6):
            at = slot * HEADS * DK + unit * width
            to = (unit % 2) * 6 * width + slot * width
            dst = (first_ref, second_ref)[unit // 2]
            dst[:, to : to + width] = w_ref[:, at : at + width]
    first_ref[:, 12 * width :] = small_ref[...]
    second_ref[:, 12 * width :] = out_ref[...]


def sort_weights(w_in, w_small, w_out):
    rows = w_in.shape[0]
    wide = 12 * LU * DK
    return pl.pallas_call(
        sort_body,
        out_shape=[
            jax.ShapeDtypeStruct((rows, wide + DK), bf16),
            jax.ShapeDtypeStruct((rows, wide + w_out.shape[1]), bf16),
        ],
        compiler_params=pltpu.CompilerParams(vmem_limit_bytes=48 << 20),
        name="sort_weights",
    )(w_in, w_small, w_out)


def natural_columns(parts):
    width = LU * DK
    count = parts[0].shape[1] // width
    return jnp.concatenate(
        [p[:, j * width : (j + 1) * width] for j in range(count) for p in parts], axis=1
    )


def all_sum(vec, total):
    axes = ("rep", "shard")
    step = 1
    while step < total:
        vec = vec + lax.ppermute(vec, axes, [(i, i ^ step) for i in range(total)])
        step *= 2
    return vec


def swap(x, axis, count, bit):
    return lax.ppermute(x, axis, [(i, i ^ bit) for i in range(count)])


def pick(blocks, index):
    return lax.dynamic_index_in_dim(blocks, index, 0, keepdims=False)


def tie(x, *deps):
    return lax.optimization_barrier((x,) + deps)[0]


def scatter(grad):
    return lax.psum_scatter(grad, "shard", scatter_dimension=0, tiled=True)


def gather(w):
    return lax.all_gather(w, "shard", axis=0, tiled=True)


def pair_body(added, idx_ref, a_ref, b_ref, g_ref, *refs):
    ins, outs = refs[: 2 * added], refs[2 * added :]
    g = g_ref[...]
    for k, lhs in enumerate((a_ref, b_ref)):
        out = tn(lhs[...], g)
        if added:
            out = out + ins[k][...].astype(f32)
        outs[k][...] = lo(out)


def grad_pair(lhs, g, idx, added=()):
    rows, wide = lhs.shape
    block = wide // 4
    cols = g.shape[1]
    tile = 512 if cols % 512 == 0 else 256
    out = jax.ShapeDtypeStruct((block, cols), bf16)
    flat = pl.BlockSpec((block, tile), lambda j, idx: (0, j))
    return pl.pallas_call(
        functools.partial(pair_body, len(added) // 2),
        grid_spec=pltpu.PrefetchScalarGridSpec(
            num_scalar_prefetch=1,
            grid=(cols // tile,),
            in_specs=[
                pl.BlockSpec((rows, block), lambda j, idx: (0, idx[0])),
                pl.BlockSpec((rows, block), lambda j, idx: (0, idx[1])),
                pl.BlockSpec((rows, tile), lambda j, idx: (0, j)),
            ]
            + [flat] * len(added),
            out_specs=[flat, flat],
        ),
        out_shape=[out, out],
        compiler_params=pltpu.CompilerParams(vmem_limit_bytes=48 << 20),
        cost_estimate=pl.CostEstimate(
            flops=100_000_000, transcendentals=0, bytes_accessed=300_000
        ),
        name="grad_pair",
    )(idx, lhs, lhs, g, *added)


def ends(me, bits):
    return jnp.stack([me ^ b for b in bits]).astype(jnp.int32)


def project_body(idx_ref, *refs):
    lhs, rhs, out = refs[:4], refs[4:8], refs[8]
    total = nn(lhs[0][...], rhs[0][...])
    for a, b in zip(lhs[1:], rhs[1:]):
        total = total + nn(a[...], b[...])
    out[...] = total


def project(x, pieces):
    me = lax.axis_index("shard")
    rows, wide = x.shape
    block, cols = pieces[0].shape
    tile = 640
    pick_lhs = lambda p: pl.BlockSpec((rows, block), lambda j, idx: (0, idx[p]))
    return pl.pallas_call(
        project_body,
        grid_spec=pltpu.PrefetchScalarGridSpec(
            num_scalar_prefetch=1,
            grid=(cols // tile,),
            in_specs=[pick_lhs(p) for p in range(4)]
            + [pl.BlockSpec((block, tile), lambda j, idx: (0, j))] * 4,
            out_specs=pl.BlockSpec((rows, tile), lambda j, idx: (0, j)),
        ),
        out_shape=jax.ShapeDtypeStruct((rows, cols), f32),
        compiler_params=pltpu.CompilerParams(vmem_limit_bytes=48 << 20),
        name="project",
    )(ends(me, (0, 1, 2, 3)), x, x, x, x, *pieces)


def pull_first_body(idx_ref, g_ref, small_ref, *refs):
    pieces, out = refs[:4], refs[4]
    block, cols = pieces[0].shape
    wide = g_ref.shape[1]
    for p in range(4):
        w = pieces[p]
        part = nt(g_ref[...], w[:, 0:wide]) + nt(small_ref[...], w[:, wide:cols])
        out[:, pl.ds(pl.multiple_of(idx_ref[p] * block, block), block)] = part


def pull_first(g, small, pieces):
    me = lax.axis_index("shard")
    rows, wide = g.shape
    tile = 256
    whole = pl.BlockSpec(pieces[0].shape, lambda i, idx: (0, 0), pipeline_mode=pl.Buffered(1))
    width = 4 * pieces[0].shape[0]
    return pl.pallas_call(
        pull_first_body,
        grid_spec=pltpu.PrefetchScalarGridSpec(
            num_scalar_prefetch=1,
            grid=(rows // tile,),
            in_specs=[
                pl.BlockSpec((tile, wide), lambda i, idx: (i, 0)),
                pl.BlockSpec((tile, small.shape[1]), lambda i, idx: (i, 0)),
            ]
            + [whole] * 4,
            out_specs=pl.BlockSpec((tile, width), lambda i, idx: (i, 0)),
        ),
        out_shape=jax.ShapeDtypeStruct((rows, width), f32),
        compiler_params=pltpu.CompilerParams(vmem_limit_bytes=48 << 20),
        name="pull_first",
    )(ends(me, (0, 1, 2, 3)), g, small, *pieces)


def pull_second_body(count, *refs):
    gs, (w_ref, part_ref, h_ref, res_ref, gain_ref, out_ref, acc_ref) = refs[:count], refs[count:]
    grad = part_ref[...]
    at = 0
    for g in gs:
        wide = g.shape[1]
        grad = grad + nt(g[...], w_ref[:, at : at + wide])
        at += wide
    h = h_ref[...].astype(f32)
    r = lax.rsqrt(jnp.mean(h * h, axis=-1, keepdims=True) + EPS)
    u = grad * gain_ref[...]
    back = r * u - (r * r * r) * h * jnp.mean(u * h, axis=-1, keepdims=True)
    out_ref[...] = lo(res_ref[...] + back)

    @pl.when(pl.program_id(0) == 0)
    def _():
        acc_ref[...] = jnp.zeros_like(acc_ref)

    t = grad * h * r
    acc_ref[...] += jnp.sum(t.reshape(t.shape[0] // 8, 8, t.shape[1]), axis=0)


def pull_second(gs, w, part, hidden, residual, gain):
    rows, width = hidden.shape
    tile = 256
    wide = sum(g.shape[1] for g in gs)
    row = lambda cols: pl.BlockSpec((tile, cols), lambda i: (i, 0))
    return pl.pallas_call(
        functools.partial(pull_second_body, len(gs)),
        grid=(rows // tile,),
        in_specs=[row(g.shape[1]) for g in gs]
        + [
            pl.BlockSpec((w.shape[0], wide), lambda i: (0, 0), pipeline_mode=pl.Buffered(1)),
            row(width),
            row(width),
            row(width),
            pl.BlockSpec((1, width), lambda i: (0, 0)),
        ],
        out_specs=[row(width), pl.BlockSpec((8, width), lambda i: (0, 0))],
        out_shape=[
            jax.ShapeDtypeStruct((rows, width), bf16),
            jax.ShapeDtypeStruct((8, width), f32),
        ],
        compiler_params=pltpu.CompilerParams(vmem_limit_bytes=56 << 20),
        name="pull_second",
    )(*gs, w, part, hidden, residual, gain.reshape(1, width))


def first_half(lhs, g):
    me = lax.axis_index("shard")
    near, far = grad_pair(lhs, g, ends(me, (1, 3)))
    return near, swap(near, "shard", 4, 1), swap(far, "shard", 4, 1)


def second_half(lhs, g, got):
    me = lax.axis_index("shard")
    part, own = grad_pair(lhs, g, ends(me, (2, 0)), (got[1], got[0]))
    return part, own, swap(part, "shard", 4, 2)


def rep_stages(own, across, late):
    rows, cols = own.shape
    me = lax.axis_index("rep")
    low = me & 1
    high = me >> 1
    own2 = own.reshape(2, rows // 2, cols)
    across2 = tie(across, late[0]).reshape(2, rows // 2, cols)
    both = lambda i: pick(own2, i).astype(f32) + pick(across2, i).astype(f32)
    send = lo(both(1 - low))
    other = swap(send, "rep", 8, 1)
    yield send
    other = tie(other, late[0])
    half = lo(both(low) + other.astype(f32)).reshape(4, rows // 8, cols)
    cuts = [pick(half, high ^ d) for d in (1, 2, 3)]
    got = [swap(c, "rep", 8, 2 * d) for c, d in zip(cuts, (1, 2, 3))]
    yield half
    got[0] = tie(got[0], late[0])
    piece = pick(half, high).astype(f32)
    for v in got:
        piece = piece + v.astype(f32)
    piece = lo(piece)
    pieces = [swap(piece, "rep", 8, 2 * d) for d in (1, 2, 3)]
    yield piece
    pieces = jnp.stack([piece, tie(pieces[0], late[0])] + pieces[1:])
    half = jnp.concatenate([pick(pieces, high ^ k) for k in range(4)], axis=0)
    other = swap(half, "rep", 8, 1)
    yield half
    both2 = jnp.stack([half, tie(other, late[0])])
    yield jnp.concatenate([pick(both2, low), pick(both2, low ^ 1)], axis=0)


def shards(
    rep_count,
    shard_count,
    hidden_in,
    teacher,
    cotangent,
    lengths,
    norm_attn,
    w_in,
    w_small,
    conv_w,
    a_log,
    dt_bias,
    norm_head,
    w_out,
    norm_mlp,
    w_mlp_in,
    w_mlp_down,
):
    row_count, width = hidden_in.shape
    seq_here = lengths.shape[0]
    slot_count = row_count // seq_here
    small_width = w_small.shape[1]
    total = rep_count * shard_count
    plain = shard_count == 4 and rep_count == 8
    unit_width = 6 * LU * DK
    part_width = 2 * unit_width
    w_small_pad = jnp.pad(w_small, ((0, 0), (0, 128 - small_width)))
    first, second = sort_weights(w_in, w_small_pad, w_out)
    if plain:
        crossed = swap(first, "shard", 4, 2)
        near = swap(first, "shard", 4, 1)
        pieces = (first, near, crossed, swap(crossed, "shard", 4, 1))
    else:
        w_first = gather(first)
    second_all = gather(second)
    w_second = second_all[:, :part_width]
    w_out_all = second_all[:, part_width:]
    w_mlp_in_all = gather(w_mlp_in)
    w_down_all = gather(w_mlp_down)

    hidden32 = hidden_in.astype(f32)
    r_in = lax.rsqrt(jnp.mean(hidden32 * hidden32, axis=-1, keepdims=True) + EPSILON)
    normed_low = (hidden32 * r_in * norm_attn).astype(bf16)
    if plain:
        proj_first = project(normed_low, pieces)
    else:
        proj_first = dot_plain(normed_low, w_first)
    head_gain = norm_head.reshape(1, DK)
    pad_lanes = ((16, 104),)
    decay_par = jnp.concatenate(
        [
            jnp.pad(-jnp.exp(a_log), pad_lanes).reshape(1, 128),
            jnp.pad(dt_bias, pad_lanes).reshape(1, 128),
            jnp.zeros((6, 128), f32),
        ],
        axis=0,
    )
    gate_at = part_width // 128
    colg, rowg = gate_fwd(proj_first, decay_par, BLOCK, at=gate_at)
    kept_first = mixer_fwd(proj_first, conv_w, colg, rowg, head_gain, seq_here, 0, 4, BLOCK, 4)
    proj_second = dot_plain(tie(normed_low, kept_first[0]), w_second)
    kept_second = mixer_fwd(
        proj_second, conv_w, colg, rowg, head_gain, seq_here, 4, 4, BLOCK, 4, kept_first[0]
    )
    mixed_low = kept_second[0]
    residual = hidden32 + dot_plain(mixed_low, w_out_all)
    r_mid = lax.rsqrt(jnp.mean(residual * residual, axis=-1, keepdims=True) + EPSILON)
    mid_low = (residual * r_mid * norm_mlp).astype(bf16)
    gate_up = dot_plain(mid_low, w_mlp_in_all)
    unit_count = w_down_all.shape[0]
    gate_part = gate_up[:, :unit_count]
    up_part = gate_up[:, unit_count:]
    sigmoid_gate = jax.nn.sigmoid(gate_part)
    silu_gate = gate_part * sigmoid_gate
    product_low = (silu_gate * up_part).astype(bf16)
    output32 = residual + dot_plain(product_low, w_down_all)
    slot_index = lax.broadcasted_iota(jnp.int32, (seq_here, slot_count), 1)
    valid_rows = (slot_index < lengths[:, None]).astype(f32).reshape(row_count, 1)
    deviation = output32 - teacher.astype(f32)
    loss_sum = jnp.sum(valid_rows * deviation * deviation)
    valid_count = jnp.sum(lengths).astype(f32)
    grad_out = valid_rows * (cotangent.astype(f32) + deviation)
    grad_out_low = grad_out.astype(bf16)

    grad_w_down = dot_left_t(product_low, grad_out_low).astype(bf16)
    own_down = scatter(grad_w_down)
    grad_product = dot_right_t(tie(grad_out_low, grad_w_down), w_down_all)
    grad_gate = grad_product * up_part * sigmoid_gate * (1.0 + gate_part * (1.0 - sigmoid_gate))
    grad_up = grad_product * silu_gate
    grad_gate_up = jnp.concatenate([grad_gate, grad_up], axis=1).astype(bf16)
    if plain:
        mlp_near, *mlp_got = first_half(mid_low, grad_gate_up)
        grad_mid = dot_right_t(tie(grad_gate_up, mlp_near), w_mlp_in_all)
        mlp_part, mlp_own, mlp_across = second_half(
            mid_low, tie(grad_gate_up, grad_mid), mlp_got
        )
        grad_mid, own_down = lax.optimization_barrier((tie(grad_mid, mlp_part), own_down))
        own_down = lax.psum(own_down, "rep")
    else:
        grad_w_mlp_in = dot_left_t(mid_low, grad_gate_up).astype(bf16)
        own_mlp_in = scatter(grad_w_mlp_in)
        grad_mid = dot_right_t(tie(grad_gate_up, grad_w_mlp_in), w_mlp_in_all)
    u_mid = grad_mid * norm_mlp
    grad_norm_mlp = jnp.sum(grad_mid * residual * r_mid, axis=0)
    grad_residual = (
        grad_out
        + r_mid * u_mid
        - (r_mid * r_mid * r_mid) * residual * jnp.mean(u_mid * residual, axis=-1, keepdims=True)
    )
    grad_res_low = grad_residual.astype(bf16)
    grad_mixed = dot_right_t(grad_res_low, w_out_all)
    if plain:
        out_near, *out_got = first_half(mixed_low, tie(grad_res_low, grad_mixed))
        deps = [out_near]
    else:
        grad_w_out = dot_left_t(mixed_low, grad_res_low).astype(bf16)
        own_out = scatter(grad_w_out)
        deps = [grad_w_out]

    projs = (proj_first, proj_second)
    kept = (kept_first, kept_second)
    pulled = []
    running = {}
    finals = {}

    late = [None]

    def advance(keys, dep):
        late[0] = dep
        outs = []
        for key in keys:
            value = next(running[key], None)
            if value is not None:
                finals[key] = value
                outs.append(value)
        return outs

    for index, (head, count) in enumerate(((0, 4), (4, 2), (6, 2))):
        half = head // 4
        if index == 1 and plain:
            own_mlp_in = lo(mlp_own.astype(f32) + tie(mlp_across, *deps).astype(f32))
            own_mlp_in, own_down = lax.optimization_barrier((own_mlp_in, own_down))
            deps = deps + [own_mlp_in]
            own_mlp_in = lax.psum(own_mlp_in, "rep")
        back = mixer_bwd(
            projs[half], conv_w, colg, rowg, head_gain, tie(grad_mixed, *deps),
            *kept[half][1:], seq_here, head, (head % 4) // count, BLOCK, count,
        )
        pulled.append(back)
        gx = back[0]
        if not plain:
            grad = dot_left_t(normed_low, gx).astype(bf16)
            finals[index] = lax.psum(scatter(grad), "rep")
            deps = [grad]
            continue
        if index == 0:
            gx = tie(gx, own_down)
        near, *got = first_half(normed_low, gx)
        outs = [near]
        if index == 0:
            out_part, out_own, out_across = second_half(
                mixed_low, tie(grad_res_low, near), out_got
            )
            outs.append(out_part)
        if index == 2:
            outs += advance([0], near)
        part, own, across = second_half(normed_low, tie(gx, *outs), got)
        if index == 0:
            own = jnp.concatenate([own, out_own], axis=1)
            across = jnp.concatenate([across, out_across], axis=1)
        running[index] = rep_stages(own, across, late)
        deps = [part]
    if not plain:
        own_down, own_mlp_in, own_out = lax.psum((own_down, own_mlp_in, own_out), "rep")
    cols = tuple(p[1] for p in pulled)
    rows = tuple(p[2] for p in pulled)
    col_last = tie(cols[-1], own_mlp_in, *deps)
    grad_small_low, gate_sums = gate_bwd(
        proj_first, decay_par, colg, cols[:-1] + (col_last,), rows, BLOCK, at=gate_at
    )
    grad_w_small = dot_left_t(grad_small_low, normed_low)[:small_width]
    gxs = [p[0] for p in pulled]

    def checkpoint(value, keys):
        if not plain:
            return value
        return tie(value, *advance(keys, value))

    gx_zero = checkpoint(tie(gxs[0], grad_small_low), [0, 1])
    if plain:
        grad_part = pull_first(gx_zero, grad_small_low, pieces)
    else:
        grad_part = dot_right_t(gx_zero, w_first[:, :part_width]) + dot_right_t(
            grad_small_low, w_first[:, part_width:]
        )
    gx_one = checkpoint(tie(gxs[1], grad_part), [0, 1, 2])
    grad_hidden, attn_part = pull_second(
        (gx_one, gxs[2]), second_all, grad_part, hidden_in, grad_residual, norm_attn
    )
    grad_norm_attn = checkpoint(jnp.sum(attn_part, axis=0), [0, 1, 2])
    grad_conv = sum(jnp.sum(p[3], axis=1) for p in pulled)
    grad_gain = sum(jnp.sum(p[4], axis=(0, 1)) for p in pulled)
    parts = (
        grad_conv.reshape(-1),
        grad_w_small.reshape(-1),
        grad_norm_mlp,
        grad_gain,
        jnp.sum(gate_sums[8:, 16:24], axis=0),
        jnp.sum(gate_sums[:8, 16:24], axis=0),
        loss_sum.reshape(1),
        valid_count.reshape(1),
        jnp.zeros((110,), f32),
    )
    packed = jnp.concatenate(parts).reshape(-1, 128)
    packed = all_sum(packed, total).reshape(-1)
    sums = []
    start = 0
    for part in parts:
        sums.append(packed[start : start + part.shape[0]])
        start += part.shape[0]
    sum_attn = all_sum(grad_norm_attn.reshape(-1, 128), total).reshape(-1)
    own_rows = w_small.shape[0]
    own_small = lax.dynamic_slice_in_dim(
        sums[1].reshape(small_width, width), lax.axis_index("shard") * own_rows, own_rows, 1
    )
    loss_value = sums[6][0] / (sums[7][0] * width)
    if plain:
        late[0] = grad_norm_attn
        for key in (0, 1, 2):
            for value in running[key]:
                finals[key] = value
        own_out = finals[0][:, part_width:]
    units = [finals[0][:, :unit_width], finals[0][:, unit_width:part_width], finals[1], finals[2]]
    return (
        output32.astype(bf16),
        loss_value,
        grad_hidden,
        sum_attn,
        natural_columns(units).astype(f32),
        own_small.T,
        sums[0].reshape(conv_w.shape),
        sums[4],
        sums[5],
        sums[3],
        own_out.astype(f32),
        sums[2],
        own_mlp_in.astype(f32),
        own_down.astype(f32),
    )


def solution(mesh):
    in_specs = (
        P(("rep", "shard"), None),
        P(("rep", "shard"), None),
        P(("rep", "shard"), None),
        P(("rep", "shard")),
        P(),
        P("shard", None),
        P("shard", None),
        P(),
        P(),
        P(),
        P(),
        P("shard", None),
        P(),
        P("shard", None),
        P("shard", None),
    )
    out_specs = (
        P(("rep", "shard"), None),
        P(),
        P(("rep", "shard"), None),
        P(),
        P("shard", None),
        P("shard", None),
        P(),
        P(),
        P(),
        P(),
        P("shard", None),
        P(),
        P("shard", None),
        P("shard", None),
    )
    return jax.shard_map(
        functools.partial(shards, mesh.shape["rep"], mesh.shape["shard"]),
        mesh=mesh,
        in_specs=in_specs,
        out_specs=out_specs,
        check_vma=False,
    )
```
